32 devices in a mesh: rows: 8 (over z, x), scales: 4 (over y, core).
Axes of the slice: x: 2, y: 2, z: 4, core: 2. Of those that a mesh axis runs over, the one named last changes fastest.
Arguments:
- image_now: float32 [256, 8192], P(('rows', 'scales')), may hold values from 0.1 to 4
- gradient: float32 [256, 8192], P(('rows', 'scales')), may hold values from -140 to 140
- hessian_weight: float32 [256, 8192], P(('rows', 'scales')), may hold values from 0.1 to 10
- psf_tiles: float32 [32, 256], P(('rows', 'scales')), may hold values from -0.5 to 1.7
- facet_of_row: int32 [256], P(('rows', 'scales')), may hold values from 0 to 31, never falling along the last dimension, each value on 1 to 32 neighbouring positions
- tile_slot: int32 [32], replicated, may hold values from 0 to 31, each once
- thresholds: float32 [4], replicated, may hold values from 0.2 to 2
Outputs:
- new_image: float32 [256, 8192], P(('rows', 'scales'))
The draws below stay inside these ranges and needn't reach their ends.
Inputs may be any that keep to these rules, and one draw needn't show every extreme that they name: `facet_of_row`: facet numbers never fall along the rows; every facet covers 1 to 32 rows, and some facet exactly 32. `tile_slot`: each facet's tile stands in a different row of psf_tiles, and every row holds one.
All inputs are finite; a program needn't handle non-finite values.
Results may differ from the reference program's by a relative error of at most 0.0001.
Values sent between devices are 32-bit elements; how exact they have to be, the bound alone decides.
A program may use at most 64 MiB of HBM per device.

```python
import math
import jax
import jax.numpy as jnp
import numpy as np
from jax import lax

COLS = 8192
TILE = 16
SUBITERS = 2
SCALES = 4
HEIGHT = 256
FACETS = 32
FMOST = 32


def draw_gradient(key, part):
    key_noise, key_rows, key_cols = jax.random.split(key, 3)
    position = jnp.arange(HEIGHT, dtype=jnp.float32)[:, None] / HEIGHT
    rising = jnp.exp(math.log(3.0) * position)
    row_scale = jnp.exp(jax.random.uniform(key_rows, (HEIGHT, 1), minval=0.0, maxval=math.log(10.0))) * rising
    col_scale = jnp.exp(jax.random.uniform(key_cols, (1, COLS), minval=0.0, maxval=math.log(10.0)))
    pattern = jnp.clip(jax.random.normal(key_noise, (HEIGHT, COLS)), -6.0, 6.0)
    return (0.03 * pattern * row_scale * col_scale).astype(jnp.float32)


def draw_hessian_weight(key, part):
    key_cells, key_rows = jax.random.split(key, 2)
    cells = jnp.exp(jax.random.uniform(key_cells, (HEIGHT, COLS), minval=math.log(0.1), maxval=0.0))
    row_scale = jnp.exp(jax.random.uniform(key_rows, (HEIGHT, 1), minval=0.0, maxval=math.log(10.0)))
    return (cells * row_scale).astype(jnp.float32)


def draw_psf_tiles(key, part):
    key_side, key_peak = jax.random.split(key, 2)
    centre = (jnp.arange(TILE * TILE) == TILE // 2 * TILE + TILE // 2)[None, :]
    side_lobes = 0.1 * jnp.clip(jax.random.normal(key_side, (FACETS, TILE * TILE)), -4.0, 4.0)
    peak_value = jax.random.uniform(key_peak, (FACETS, 1), minval=0.8, maxval=1.2)
    return jnp.where(centre, peak_value + side_lobes, side_lobes).astype(jnp.float32)


def level_of(key, shape, cuts, least, largest):
    def one(dim, parts):
        heights = jax.random.uniform(jax.random.fold_in(jax.random.fold_in(key, 6), dim), (parts,), jnp.float32, least / len(cuts), largest / len(cuts))
        return jnp.repeat(jnp.exp(heights), shape[dim] // parts).reshape((-1,) + (1,) * (len(shape) - dim - 1))

    gain = one(*cuts[0])
    for cut in cuts[1:]:
        gain = gain * one(*cut)
    return gain


def profile(number_of, total, reach, slope):
    loads = [(1 << 20) // math.isqrt(grade ** slope) + 1 for grade in range(2, number_of + 1)]
    spare, given = total - reach - (number_of - 1), [1] * (number_of - 1)
    while spare > 0:
        movable = [i for i in range(number_of - 1) if given[i] < reach]
        whole, budget = sum([loads[i] for i in movable]), spare
        for i in movable:
            extra = min(reach - given[i], max(1, budget * loads[i] // whole), spare)
            given[i] = given[i] + extra
            spare = spare - extra
    return np.array([reach] + given)


def ragged_sizes(key, count, total, bound, lean):
    if count == 2:
        one = jax.random.randint(key, (), max(1, total - bound), min(bound, total - 1) + 1)
        return jnp.stack([one, total - one])
    sizes = jnp.asarray(profile(count, total, bound, lean), jnp.int32)
    couples = (count - 1) // 2
    source_of, receiver = sizes[1:1 + 2 * couples:2], sizes[2:2 + 2 * couples:2]
    slack = jnp.minimum(source_of - 1, bound - receiver)
    moved = jax.random.randint(jax.random.fold_in(key, 1), (couples,), 0, 1 << 20) % (slack + 1)
    sizes = sizes.at[1:1 + 2 * couples:2].set(source_of - moved).at[2:2 + 2 * couples:2].set(receiver + moved)
    return sizes[jax.random.permutation(jax.random.fold_in(key, 2), count)]


def setup_inputs(seed: int = 0) -> dict:
    streams_of = jax.random.split(jax.random.key(seed), 8)
    return {
        "image_now": jnp.clip(jnp.exp(math.log(4.0) - 3.6888794 * jax.random.uniform(streams_of[0], (HEIGHT, COLS), jnp.float32) ** level_of(streams_of[0], (HEIGHT, COLS), ((0, 32),), -0.2, 0.2)), 0.1, 4.0),
        "gradient": draw_gradient(jax.random.fold_in(streams_of[7], 71), 0),
        "hessian_weight": draw_hessian_weight(jax.random.fold_in(streams_of[7], 71), 0),
        "psf_tiles": draw_psf_tiles(jax.random.fold_in(streams_of[7], 71), 0),
        "facet_of_row": jnp.searchsorted(jnp.cumsum(ragged_sizes(streams_of[4], FACETS, HEIGHT, FMOST, 2)), jnp.arange(HEIGHT), side="right").astype(jnp.int32),
        "tile_slot": jax.random.permutation(streams_of[5], FACETS).astype(jnp.int32),
        "thresholds": jnp.clip(jnp.exp(jax.random.uniform(streams_of[6], (SCALES,), jnp.float32, math.log(0.2), math.log(2.0))), 0.2, 2.0),
    }


SPLINE_EDGE = 0.0625
SPLINE_NEAR = 0.25
SPLINE_MID = 0.375


def along_columns(source, spacing):
    length = source.shape[1]
    padded = jnp.pad(source, ((0, 0), (2 * spacing, 2 * spacing)))
    outer_pair = padded[:, 0:length] + padded[:, 4 * spacing:4 * spacing + length]
    inner_pair = padded[:, spacing:spacing + length] + padded[:, 3 * spacing:3 * spacing + length]
    return SPLINE_EDGE * outer_pair + SPLINE_NEAR * inner_pair + SPLINE_MID * source


def along_rows(source, spacing):
    length = source.shape[0]
    padded = jnp.pad(source, ((2 * spacing, 2 * spacing), (0, 0)))
    outer_pair = padded[0:length] + padded[4 * spacing:4 * spacing + length]
    inner_pair = padded[spacing:spacing + length] + padded[3 * spacing:3 * spacing + length]
    return SPLINE_EDGE * outer_pair + SPLINE_NEAR * inner_pair + SPLINE_MID * source


def forward_blur(source, weights):
    height, columns = source.shape
    half_tile = TILE // 2
    padded = jnp.pad(source, ((half_tile, half_tile), (half_tile, half_tile)))

    def add_tap_row(tap_row, summed):
        shifted = lax.dynamic_slice_in_dim(padded, tap_row, height, 0)
        tap_weights = lax.dynamic_index_in_dim(weights, tap_row, 1, keepdims=False)
        for column in range(TILE):
            summed = summed + tap_weights[:, column:column + 1] * shifted[:, column:column + columns]
        return summed

    return lax.fori_loop(0, TILE, add_tap_row, jnp.zeros((height, columns), jnp.float32))


def adjoint_blur(source, weights):
    height, columns = source.shape
    half_tile = TILE // 2
    padded = jnp.pad(source, ((half_tile, half_tile), (half_tile, half_tile)))
    wide_weights = jnp.pad(weights, ((half_tile, half_tile), (0, 0), (0, 0)))

    def add_tap_row(tap_row, summed):
        offset = 2 * half_tile - tap_row
        shifted = lax.dynamic_slice_in_dim(padded, offset, height, 0)
        weight_rows = lax.dynamic_slice_in_dim(wide_weights, offset, height, 0)
        tap_weights = lax.dynamic_index_in_dim(weight_rows, tap_row, 1, keepdims=False)
        for column in range(TILE):
            offset_col = 2 * half_tile - column
            summed = summed + tap_weights[:, column:column + 1] * shifted[:, offset_col:offset_col + columns]
        return summed

    return lax.fori_loop(0, TILE, add_tap_row, jnp.zeros((height, columns), jnp.float32))


def shrink(trial, step_size, thresholds):
    smooth = trial
    summed = jnp.zeros_like(trial)
    for depth in range(SCALES):
        smoother = along_rows(along_columns(smooth, 2 ** depth), 2 ** depth)
        detail = smooth - smoother
        limit = step_size * thresholds[depth]
        summed = summed + (detail - jnp.clip(detail, -limit, limit))
        smooth = smoother
    return summed + smooth


def reference(image_now, gradient, hessian_weight, psf_tiles, facet_of_row, tile_slot, thresholds):
    slot_rows = jnp.take(tile_slot, facet_of_row).astype(jnp.int32)
    weights = jnp.take(psf_tiles, slot_rows, axis=0).reshape(HEIGHT, TILE, TILE)
    current = image_now
    for sweep in range(SUBITERS):
        change = current - image_now
        pushed = hessian_weight * forward_blur(change, weights)
        descent = gradient + adjoint_blur(pushed, weights)
        blurred = forward_blur(descent, weights)
        step_size = jnp.sum(descent * descent) / jnp.sum(hessian_weight * blurred * blurred)
        current = shrink(current - step_size * descent, step_size, thresholds)
    return current
```

```python
import functools

import jax
import jax.numpy as jnp
import numpy as np
from jax import lax
from jax.experimental import pallas as pl
from jax.experimental.pallas import tpu as pltpu
from jax.sharding import PartitionSpec as P

TILE = 16
HALF = TILE // 2
SUBITERS = 2
LANES = 128
BLOCK = 32
GROUPS = LANES // BLOCK
WIDTH = 8 * BLOCK
AXES = ("rows", "scales")
VMEM = pl.BlockSpec(memory_space=pltpu.VMEM)


def spline_matrices(levels):
    w = np.arange(WIDTH)
    same = (w[:, None] // BLOCK) == (w[None, :] // BLOCK)
    offset = (w[:, None] % BLOCK) - (w[None, :] % BLOCK)
    planes = []
    for level in range(levels):
        d = 2**level
        for s in (-1, 0, 1):
            o = np.abs(offset + BLOCK * s)
            coef = np.where(o == 0, 0.375, np.where(o == d, 0.25, np.where(o == 2 * d, 0.0625, 0.0)))
            planes.append(np.where(same, coef, 0.0))
    return jnp.asarray(np.stack(planes), jnp.bfloat16)


def halves(x):
    high = x.astype(jnp.bfloat16)
    low = (x - high.astype(jnp.float32)).astype(jnp.bfloat16)
    return high, low


def dot(a, b):
    return jnp.dot(a, b, preferred_element_type=jnp.float32)


def block_shift(x, s):
    if s == 0:
        return x
    count = x.shape[0] // GROUPS
    parts = [x[p * count : (p + 1) * count] for p in range(GROUPS)]
    row = lax.broadcasted_iota(jnp.int32, parts[0].shape, 0)
    if s == 1:
        last = jnp.where(row == count - 1, 0.0, pltpu.roll(parts[0], count - 1, 0))
        return jnp.concatenate(parts[1:] + [last], axis=0)
    first = jnp.where(row == 0, 0.0, pltpu.roll(parts[-1], 1, 0))
    return jnp.concatenate([first] + parts[:-1], axis=0)


def blur(stripes, high_ref, low_ref):
    total = None
    for t, x in enumerate(stripes):
        for s in (-1, 0, 1):
            high, low = halves(block_shift(x, s))
            n = t * 3 + s + 1
            w = high_ref[n]
            part = dot(high, w) + dot(low, w) + dot(high, low_ref[n])
            total = part if total is None else total + part
    return total


def to_blocks(src_ref, dst_ref, tiles):
    count = src_ref.shape[1] // LANES
    for q in range(count):
        tiles[pl.ds(8 * q, 8), :] = src_ref[:, q * LANES : (q + 1) * LANES]
    group = lax.broadcasted_iota(jnp.int32, (count, LANES), 1) // BLOCK
    for half in range(2):
        outs = [None] * GROUPS
        for k in range(4):
            a = tiles[pl.ds(half * 4 + k, count, stride=8), :]
            for p in range(GROUPS):
                shift = BLOCK * ((k - p) % 4)
                moved = pltpu.roll(a, shift, 1) if shift else a
                outs[p] = moved if k == 0 else jnp.where(group == k, moved, outs[p])
        for p in range(GROUPS):
            dst_ref[p * count : (p + 1) * count, half * LANES : (half + 1) * LANES] = outs[p]


def from_blocks(src_ref, dst_ref, tiles):
    count = dst_ref.shape[1] // LANES
    group = lax.broadcasted_iota(jnp.int32, (count, LANES), 1) // BLOCK
    for half in range(2):
        for k in range(4):
            out = None
            for p in range(GROUPS):
                x = src_ref[p * count : (p + 1) * count, half * LANES : (half + 1) * LANES]
                shift = BLOCK * ((p - k) % 4)
                moved = pltpu.roll(x, shift, 1) if shift else x
                out = moved if p == 0 else jnp.where(group == p, moved, out)
            tiles[pl.ds(half * 4 + k, count, stride=8), :] = out
    for q in range(count):
        dst_ref[:, q * LANES : (q + 1) * LANES] = tiles[pl.ds(8 * q, 8), :]


def build_weights(base_ref, lead, high_ref, low_ref, wide):
    lane = lax.broadcasted_iota(jnp.int32, (8, WIDTH), 1) % BLOCK
    for t in range(3):
        base = base_ref[8 * t : 8 * t + 8, :]
        for w in range(BLOCK):
            for s in (-1, 0, 1):
                moved = pltpu.roll(base, (w - lead + BLOCK * s) % WIDTH, 1)
                x = lane - (w - lead + BLOCK * s)
                kept = jnp.where((x >= 0) & (x < TILE), moved, 0.0)
                for half in range(2):
                    wide[s + 1, half, pl.ds(w, 8, stride=BLOCK), :] = kept[
                        :, half * LANES : (half + 1) * LANES
                    ]
        for s in range(3):
            for half in range(2):
                high, low = halves(wide[s, half])
                high_ref[t * 3 + s, :, half * LANES : (half + 1) * LANES] = high
                low_ref[t * 3 + s, :, half * LANES : (half + 1) * LANES] = low


def moved_rows(vregs, rolls, i, d):
    if d % 4 == 0:
        return vregs[i + d // 4]
    shift = (-BLOCK * d) % LANES

    def rolled(n):
        if (n, shift) not in rolls:
            rolls[(n, shift)] = pltpu.roll(vregs[n], shift, 1)
        return rolls[(n, shift)]

    lane = lax.broadcasted_iota(jnp.int32, vregs[i].shape, 1)
    if d > 0:
        return jnp.where(lane < LANES - BLOCK * d, rolled(i), rolled(i + 1))
    return jnp.where(lane >= -BLOCK * d, rolled(i), rolled(i - 1))


def column_cascade(stripe_refs, alive, levels_ref, step_rows):
    reach = len(stripe_refs) // 2
    levels = levels_ref.shape[0]

    def chunk(n, carry):
        rows = pl.ds(pl.multiple_of(n * step_rows, step_rows), step_rows)
        vregs = {}
        for t, ref in enumerate(stripe_refs):
            for half in range(2):
                vregs[2 * t + half] = ref[rows, half * LANES : (half + 1) * LANES]
        own = 2 * reach
        for level in range(levels):
            d = 2**level
            left = 2 ** (levels + 1) - 2 ** (level + 2)
            margin = -(-left // 4)
            rolls, out = {}, {}
            keys = vregs
            for i in range(own - margin, own + 2 + margin):
                outer = moved_rows(keys, rolls, i, -2 * d) + moved_rows(keys, rolls, i, 2 * d)
                inner = moved_rows(keys, rolls, i, -d) + moved_rows(keys, rolls, i, d)
                value = 0.0625 * outer + 0.25 * inner + 0.375 * keys[i]
                t = i // 2
                out[i] = value if t == reach else value * alive[t]
            vregs = out
            for half in range(2):
                levels_ref[level, rows, half * LANES : (half + 1) * LANES] = out[own + half]
        return carry

    lax.fori_loop(0, stripe_refs[0].shape[0] // step_rows, chunk, 0)


def row_cascade(levels_ref, spline_ref):
    levels = levels_ref.shape[0]
    for level in range(levels):

        def one(k, carry):
            x = levels_ref[k]
            total = None
            for s in (-1, 0, 1):
                high, low = halves(block_shift(x, s))
                w = spline_ref[level * 3 + s + 1]
                part = dot(high, w) + dot(low, w)
                total = part if total is None else total + part
            levels_ref[k] = total
            return carry

        lax.fori_loop(level, levels, one, 0)


def keep(own, levels_ref, limits):
    levels = levels_ref.shape[0]
    smooth = own
    total = None
    for k in range(levels):
        smoother = levels_ref[k]
        detail = smooth - smoother
        part = detail - jnp.clip(detail, -limits[k], limits[k])
        total = part if total is None else total + part
        smooth = smoother
    return total + smooth


def prepare_kernel(image, gradient, weight, base_f, base_a, xi, xg, xh, fh, fl, ah, al, tiles, wide):
    to_blocks(image, xi, tiles)
    to_blocks(gradient, xg, tiles)
    to_blocks(weight, xh, tiles)
    build_weights(base_f, HALF - 1, fh, fl, wide)
    build_weights(base_a, HALF, ah, al, wide)


def forward_kernel(below, own, above, h, fh, fl, out):
    out[...] = h[...] * blur([below[...], own[...], above[...]], fh, fl)


def adjoint_kernel(below, own, above, g, ah, al, out):
    out[...] = g[...] + blur([below[...], own[...], above[...]], ah, al)


def sums_kernel(below, own, above, h, fh, fl, out):
    d = own[...]
    b = blur([below[...], d, above[...]], fh, fl)
    first = jnp.sum(d * d, axis=0, keepdims=True)
    second = jnp.sum(h[...] * b * b, axis=0, keepdims=True)
    out[...] = jnp.concatenate([first, second], axis=0)


def shrink_kernel(*refs, count, final):
    stripes, alive_ref, limits_ref, spline = refs[:count], refs[count], refs[count + 1], refs[count + 2]
    out, levels = refs[count + 3], refs[count + 4]
    alive = [alive_ref[t] for t in range(count)]
    column_cascade(stripes, alive, levels, 8)
    row_cascade(levels, spline)
    new = keep(stripes[count // 2][...], levels, [limits_ref[k] for k in range(levels.shape[0])])
    if final:
        whole, tiles = refs[count + 5], refs[count + 6]
        whole[...] = new
        from_blocks(whole, out, tiles)
    else:
        out[...] = new


def call(kernel, outs, *args, scratch=(), smem=()):
    specs = [pl.BlockSpec(memory_space=pltpu.SMEM) if n in smem else VMEM for n in range(len(args))]
    many = isinstance(outs, list)
    return pl.pallas_call(
        kernel,
        out_shape=outs,
        in_specs=specs,
        out_specs=[VMEM] * len(outs) if many else VMEM,
        scratch_shapes=list(scratch),
        compiler_params=pltpu.CompilerParams(vmem_limit_bytes=56 * 1024 * 1024),
    )(*args)


def bases(taps, wide_taps):
    rows = taps.shape[0]
    flipped = jnp.flip(taps, axis=2)
    forward = jnp.stack([jnp.pad(flipped[r], ((r, rows - r), (0, 0))) for r in range(rows)], axis=1)
    padded = jnp.pad(wide_taps, ((0, 0), (rows, rows), (0, 0)))
    adjoint = jnp.stack(
        [padded[i, 3 * rows - i : 4 * rows - i] for i in range(3 * rows)], axis=0
    )
    widen = lambda x: jnp.pad(x, ((0, 0), (0, 0), (0, BLOCK - TILE))).reshape(3 * rows, WIDTH)
    return widen(forward), widen(adjoint)


def body(image_now, gradient, hessian_weight, psf_tiles, facet_of_row, tile_slot, thresholds):
    band, columns = image_now.shape
    levels = thresholds.shape[0]
    blocks = columns // BLOCK
    count = lax.axis_size("rows") * lax.axis_size("scales")
    me = lax.axis_index("rows") * lax.axis_size("scales") + lax.axis_index("scales")

    def from_offset(x, offset):
        pairs = [(i, i - offset) for i in range(count) if 0 <= i - offset < count]
        return lax.ppermute(x, AXES, pairs)

    facet_ids = jnp.arange(tile_slot.shape[0], dtype=jnp.int32)
    slot_rows = jnp.sum(
        jnp.where(facet_of_row[:, None] == facet_ids[None, :], tile_slot[None, :], 0), axis=1
    )
    tiles_in = lax.all_gather(psf_tiles, AXES, axis=0, tiled=True)
    length = tiles_in.shape[0]
    onehot = (slot_rows[:, None] == jnp.arange(length, dtype=jnp.int32)[None, :]).astype(jnp.float32)
    flat = jnp.dot(
        onehot, tiles_in, precision=lax.Precision.HIGHEST, preferred_element_type=jnp.float32
    )
    wide_flat = jnp.concatenate([from_offset(flat, -1), flat, from_offset(flat, 1)], axis=0)
    base_f, base_a = bases(
        flat.reshape(band, TILE, TILE), wide_flat.reshape(3 * band, TILE, TILE)
    )
    plane = jax.ShapeDtypeStruct((blocks, WIDTH), jnp.float32)
    table = jax.ShapeDtypeStruct((9, WIDTH, WIDTH), jnp.bfloat16)
    tiles = pltpu.VMEM((columns // LANES * 8, LANES), jnp.float32)
    xi, xg, xh, fh, fl, ah, al = call(
        prepare_kernel,
        [plane] * 3 + [table] * 4,
        image_now, gradient, hessian_weight, base_f, base_a,
        scratch=[tiles, pltpu.VMEM((3, 2, WIDTH, LANES), jnp.float32)],
    )
    spline = spline_matrices(levels)
    reach = 2 ** (levels + 1) - 2
    side = -(-reach // band)
    offsets = list(range(-side, side + 1))
    alive = jnp.stack([((me + o >= 0) & (me + o < count)).astype(jnp.float32) for o in offsets])

    def around(x):
        return from_offset(x, -1), x, from_offset(x, 1)

    current = xi
    for sweep in range(SUBITERS):
        if sweep == 0:
            descent = xg
        else:
            pushed = call(forward_kernel, plane, *around(current - xi), xh, fh, fl)
            descent = call(adjoint_kernel, plane, *around(pushed), xg, ah, al)
        sums = call(
            sums_kernel, jax.ShapeDtypeStruct((2, WIDTH), jnp.float32), *around(descent), xh, fh, fl
        )
        totals = lax.psum(jnp.sum(sums, axis=1), AXES)
        step_size = totals[0] / totals[1]
        trial = current - step_size * descent
        stripes = [from_offset(trial, o) if o else trial for o in offsets]
        final = sweep == SUBITERS - 1
        scratch = [pltpu.VMEM((levels, blocks, WIDTH), jnp.float32)]
        if final:
            scratch += [pltpu.VMEM((blocks, WIDTH), jnp.float32), tiles]
        n = len(stripes)
        current = call(
            functools.partial(shrink_kernel, count=n, final=final),
            jax.ShapeDtypeStruct((band, columns), jnp.float32) if final else plane,
            *stripes, alive, step_size * thresholds, spline,
            scratch=scratch, smem=(n, n + 1),
        )
    return current


def solution(mesh):
    band = P(AXES, None)
    in_specs = (band, band, band, band, P(AXES), P(), P())
    return jax.shard_map(body, mesh=mesh, in_specs=in_specs, out_specs=band, check_vma=False)
```

```python
import functools

import jax
import jax.numpy as jnp
import numpy as np
from jax import lax
from jax.experimental import pallas as pl
from jax.experimental.pallas import tpu as pltpu
from jax.sharding import PartitionSpec as P

TILE = 16
HALF = TILE // 2
SUBITERS = 2
LANES = 128
BLOCK = 32
GROUPS = LANES // BLOCK
WIDTH = 8 * BLOCK
AXES = ("rows", "scales")
VMEM = pl.BlockSpec(memory_space=pltpu.VMEM)


def spline_matrices(levels):
    w = np.arange(WIDTH)
    same = (w[:, None] // BLOCK) == (w[None, :] // BLOCK)
    offset = (w[:, None] % BLOCK) - (w[None, :] % BLOCK)
    planes = []
    for level in range(levels):
        d = 2**level
        for s in (-1, 0, 1):
            o = np.abs(offset + BLOCK * s)
            coef = np.where(o == 0, 0.375, np.where(o == d, 0.25, np.where(o == 2 * d, 0.0625, 0.0)))
            planes.append(np.where(same, coef, 0.0))
    return jnp.asarray(np.stack(planes), jnp.bfloat16)


def halves(x):
    high = x.astype(jnp.bfloat16)
    low = (x - high.astype(jnp.float32)).astype(jnp.bfloat16)
    return high, low


def dot(a, b):
    return jnp.dot(a, b, preferred_element_type=jnp.float32)


def block_shift(x, s):
    if s == 0:
        return x
    count = x.shape[0] // GROUPS
    parts = [x[p * count : (p + 1) * count] for p in range(GROUPS)]
    row = lax.broadcasted_iota(jnp.int32, parts[0].shape, 0)
    if s == 1:
        last = jnp.where(row == count - 1, 0.0, pltpu.roll(parts[0], count - 1, 0))
        return jnp.concatenate(parts[1:] + [last], axis=0)
    first = jnp.where(row == 0, 0.0, pltpu.roll(parts[-1], 1, 0))
    return jnp.concatenate([first] + parts[:-1], axis=0)


def blur(stripes, high_ref, low_ref):
    parts = [halves(x) for x in stripes]
    total = None
    for s in (-1, 0, 1):
        here = None
        for t, (high, low) in enumerate(parts):
            w = high_ref[t * 3 + s + 1]
            part = dot(high, w) + dot(low, w) + dot(high, low_ref[t * 3 + s + 1])
            here = part if here is None else here + part
        here = block_shift(here, s)
        total = here if total is None else total + here
    return total


def to_blocks(src_ref, dst_ref, tiles):
    count = src_ref.shape[1] // LANES
    for q in range(count):
        tiles[pl.ds(8 * q, 8), :] = src_ref[:, q * LANES : (q + 1) * LANES]
    group = lax.broadcasted_iota(jnp.int32, (count, LANES), 1) // BLOCK
    for half in range(2):
        outs = [None] * GROUPS
        for k in range(4):
            a = tiles[pl.ds(half * 4 + k, count, stride=8), :]
            for p in range(GROUPS):
                shift = BLOCK * ((k - p) % 4)
                moved = pltpu.roll(a, shift, 1) if shift else a
                outs[p] = moved if k == 0 else jnp.where(group == k, moved, outs[p])
        for p in range(GROUPS):
            dst_ref[p * count : (p + 1) * count, half * LANES : (half + 1) * LANES] = outs[p]


def from_blocks(src_ref, dst_ref, tiles):
    count = dst_ref.shape[1] // LANES
    group = lax.broadcasted_iota(jnp.int32, (count, LANES), 1) // BLOCK
    for half in range(2):
        for k in range(4):
            out = None
            for p in range(GROUPS):
                x = src_ref[p * count : (p + 1) * count, half * LANES : (half + 1) * LANES]
                shift = BLOCK * ((p - k) % 4)
                moved = pltpu.roll(x, shift, 1) if shift else x
                out = moved if p == 0 else jnp.where(group == p, moved, out)
            tiles[pl.ds(half * 4 + k, count, stride=8), :] = out
    for q in range(count):
        dst_ref[:, q * LANES : (q + 1) * LANES] = tiles[pl.ds(8 * q, 8), :]


def build_weights(base_ref, lead, high_ref, low_ref, wide):
    lane = lax.broadcasted_iota(jnp.int32, (8, WIDTH), 1) % BLOCK
    for t in range(3):
        base = base_ref[8 * t : 8 * t + 8, :]
        for w in range(BLOCK):
            for s in (-1, 0, 1):
                moved = pltpu.roll(base, (w - lead + BLOCK * s) % WIDTH, 1)
                x = lane - (w - lead + BLOCK * s)
                kept = jnp.where((x >= 0) & (x < TILE), moved, 0.0)
                for half in range(2):
                    wide[s + 1, half, pl.ds(w, 8, stride=BLOCK), :] = kept[
                        :, half * LANES : (half + 1) * LANES
                    ]
        for s in range(3):
            for half in range(2):
                high, low = halves(wide[s, half])
                high_ref[t * 3 + s, :, half * LANES : (half + 1) * LANES] = high
                low_ref[t * 3 + s, :, half * LANES : (half + 1) * LANES] = low


def moved_rows(vregs, rolls, i, d):
    if d % 4 == 0:
        return vregs[i + d // 4]
    shift = (-BLOCK * d) % LANES

    def rolled(n):
        if (n, shift) not in rolls:
            rolls[(n, shift)] = pltpu.roll(vregs[n], shift, 1)
        return rolls[(n, shift)]

    lane = lax.broadcasted_iota(jnp.int32, vregs[i].shape, 1)
    if d > 0:
        return jnp.where(lane < LANES - BLOCK * d, rolled(i), rolled(i + 1))
    return jnp.where(lane >= -BLOCK * d, rolled(i), rolled(i - 1))


def column_cascade(stripe_refs, alive, levels_ref, step_rows):
    reach = len(stripe_refs) // 2
    levels = levels_ref.shape[0]

    def chunk(n, carry):
        rows = pl.ds(pl.multiple_of(n * step_rows, step_rows), step_rows)
        vregs = {}
        for t, ref in enumerate(stripe_refs):
            for half in range(2):
                vregs[2 * t + half] = ref[rows, half * LANES : (half + 1) * LANES]
        own = 2 * reach
        for level in range(levels):
            d = 2**level
            left = 2 ** (levels + 1) - 2 ** (level + 2)
            margin = -(-left // 4)
            rolls, out = {}, {}
            keys = vregs
            for i in range(own - margin, own + 2 + margin):
                outer = moved_rows(keys, rolls, i, -2 * d) + moved_rows(keys, rolls, i, 2 * d)
                inner = moved_rows(keys, rolls, i, -d) + moved_rows(keys, rolls, i, d)
                value = 0.0625 * outer + 0.25 * inner + 0.375 * keys[i]
                t = i // 2
                out[i] = value if t == reach else value * alive[t]
            vregs = out
            for half in range(2):
                levels_ref[level, rows, half * LANES : (half + 1) * LANES] = out[own + half]
        return carry

    lax.fori_loop(0, stripe_refs[0].shape[0] // step_rows, chunk, 0)


def row_cascade(levels_ref, spline_ref):
    levels = levels_ref.shape[0]
    for level in range(levels):

        def one(k, carry):
            high, low = halves(levels_ref[k])
            total = None
            for s in (-1, 0, 1):
                w = spline_ref[level * 3 + s + 1]
                part = block_shift(dot(high, w) + dot(low, w), s)
                total = part if total is None else total + part
            levels_ref[k] = total
            return carry

        lax.fori_loop(level, levels, one, 0)


def keep(own, levels_ref, limits):
    levels = levels_ref.shape[0]
    smooth = own
    total = None
    for k in range(levels):
        smoother = levels_ref[k]
        detail = smooth - smoother
        part = detail - jnp.clip(detail, -limits[k], limits[k])
        total = part if total is None else total + part
        smooth = smoother
    return total + smooth


def build_bases(taps, flipped, forward, adjoint):
    lane = lax.broadcasted_iota(jnp.int32, (8, WIDTH), 1)
    sub = lax.broadcasted_iota(jnp.int32, (8, WIDTH), 0)
    group, inside = lane // BLOCK, lane % BLOCK < TILE
    own = flipped[...]
    turned = [pltpu.roll(own, TILE * n, 1) if n else own for n in range(TILE)]
    forward[...] = jnp.zeros_like(forward)
    for a in range(TILE):
        placed = jnp.zeros((8, WIDTH), jnp.float32)
        for r in range(8):
            placed = jnp.where((sub == r) & (group == r) & inside, turned[(2 * r - a) % TILE], placed)
        forward[a : a + 8, :] += placed
    for t in range(3):
        x = taps[t]
        row = sub + 8 * t
        tap = group - row + TILE
        placed = jnp.zeros((8, WIDTH), jnp.float32)
        for n in range(TILE):
            moved = pltpu.roll(x, TILE * n, 1) if n else x
            use = ((group + row) % TILE == n) & inside & (tap >= 0) & (tap < TILE)
            placed = jnp.where(use, moved, placed)
        adjoint[8 * t : 8 * t + 8, :] = placed


def kernel(
    count, scales, side,
    image, gradient, weight, psf, facet, slot_of, thresholds, spline,
    out,
    xi, xg, xh, current, near, middle, far, psf_all, taps, flipped, base_f, base_a, fh, fl, ah, al,
    levels, sums, tiles, wide,
    psf_send, psf_recv, sum_send, sum_recv, tap_send, tap_recv, near_send, near_recv, far_send, far_recv,
):
    me = lax.axis_index("rows") * scales + lax.axis_index("scales")
    barrier = pltpu.get_barrier_semaphore()

    def device(index):
        return (index // scales, index % scales)

    def peer(k):
        return (me + k) % count

    def exists(o):
        return (me + o >= 0) & (me + o < count)

    def greet(k, carry):
        pl.semaphore_signal(barrier, inc=1, device_id=device(peer(k)), device_id_type=MESH)
        return carry

    lax.fori_loop(1, count, greet, 0)

    def copy(src, dst, send_sem, recv_sem, index):
        return pltpu.make_async_remote_copy(
            src_ref=src, dst_ref=dst, send_sem=send_sem, recv_sem=recv_sem,
            device_id=device(index), device_id_type=MESH,
        )

    def share(src, pool, send, recv):
        def start(k, carry):
            copy(src, pool.at[me], send.at[k], recv.at[me], peer(k)).start()
            return carry

        lax.fori_loop(1, count, start, 0)

    def collect(src, pool, send, recv):
        def wait(k, carry):
            copy(src, pool.at[peer(k)], send.at[k], recv.at[peer(k)], peer(k)).wait()
            return carry

        lax.fori_loop(1, count, wait, 0)

    def spread(src, place, send, recv, offsets):
        for o in offsets:

            @pl.when(exists(o))
            def _():
                copy(src, place(-o), send(o), recv(-o), me + o).start()

    def arrive(src, place, send, recv, offsets):
        for o in offsets:

            @pl.when(exists(o))
            def _():
                copy(src, place(o), send(o), recv(o), me + o).wait()

    def near_spread(e, src):
        args = (src, lambda o: near.at[e, (o + 1) // 2], lambda o: near_send.at[e, (o + 1) // 2],
                lambda o: near_recv.at[e, (o + 1) // 2], (-1, 1))
        spread(*args)
        return lambda: arrive(*args)

    offsets = [sign * o for o in range(1, side + 1) for sign in (-1, 1)]

    def far_spread(e):
        args = (middle, lambda o: far.at[o + side], lambda o: far_send.at[e, o + side],
                lambda o: far_recv.at[e, o + side], offsets)
        spread(*args)
        return lambda: arrive(*args)

    to_blocks(gradient, xg, tiles)
    for o in (-1, 1):

        @pl.when(jnp.logical_not(exists(o)))
        def _():
            for e in range(near.shape[0]):
                near[e, (o + 1) // 2] = jnp.zeros(near.shape[2:], jnp.float32)
            taps[o + 1] = jnp.zeros(taps.shape[1:], jnp.float32)

    for o in offsets:

        @pl.when(jnp.logical_not(exists(o)))
        def _():
            far[o + side] = jnp.zeros(far.shape[1:], jnp.float32)

    pl.semaphore_wait(barrier, count - 1)
    share(psf, psf_all, psf_send, psf_recv)
    near_done = near_spread(0, xg)
    to_blocks(image, xi, tiles)
    to_blocks(weight, xh, tiles)
    psf_all[me] = psf[...]
    collect(psf, psf_all, psf_send, psf_recv)
    for r in range(8):
        both = psf_all[slot_of[facet[r]]]
        taps[1, r : r + 1, :] = both[0:1]
        flipped[r : r + 1, :] = both[1:2]
    tap_args = (taps.at[1], lambda o: taps.at[o + 1], lambda o: tap_send.at[(o + 1) // 2],
                lambda o: tap_recv.at[(o + 1) // 2], (-1, 1))
    spread(*tap_args)
    arrive(*tap_args)
    build_bases(taps, flipped, base_f, base_a)
    build_weights(base_f, HALF - 1, fh, fl, wide)
    alive = [None if t == side else jnp.where(exists(t - side), 1.0, 0.0) for t in range(2 * side + 1)]

    for sweep in range(SUBITERS):
        if sweep == 0:
            descent = xg
        else:
            descent = middle
            e = 3 * sweep - 2
            done = near_spread(e, current_change)
            done()
            change = current_change[...]
            pushed = xh[...] * blur([near[e, 0], change, near[e, 1]], fh, fl)
            far[side] = pushed
            near_done = near_spread(e + 1, far.at[side])
            near_done()
            middle[...] = xg[...] + blur([near[e + 1, 0], pushed, near[e + 1, 1]], ah, al)
            near_done = near_spread(e + 2, middle)
        near_done()
        e = 3 * sweep
        d = descent[...]
        b = blur([near[e, 0], d, near[e, 1]], fh, fl)

        def lanes(x):
            column = jnp.sum(x, axis=0, keepdims=True)
            return column[:, :LANES] + column[:, LANES:]

        sums[sweep, me] = jnp.concatenate([lanes(d * d), lanes(xh[...] * b * b)], axis=0)
        own = sums.at[sweep, me]
        share(own, sums.at[sweep], sum_send.at[sweep], sum_recv.at[sweep])
        if sweep == 0:
            build_weights(base_a, HALF, ah, al, wide)
        collect(own, sums.at[sweep], sum_send.at[sweep], sum_recv.at[sweep])
        totals = jnp.sum(jnp.sum(sums[sweep], axis=0), axis=1, keepdims=True)
        step = totals[0:1] / totals[1:2]
        start = xi if sweep == 0 else current
        middle[...] = start[...] - step * d
        far_done = far_spread(sweep)
        far_done()
        stripes = [middle if t == side else far.at[t] for t in range(2 * side + 1)]
        column_cascade(stripes, alive, levels, 8)
        row_cascade(levels, spline)
        new = keep(middle[...], levels, [step * thresholds[k] for k in range(levels.shape[0])])
        current[...] = new
        if sweep < SUBITERS - 1:
            current_change = far.at[side]
            current_change[...] = new - xi[...]
    from_blocks(current, out, tiles)


MESH = pl.DeviceIdType.MESH


def body(image_now, gradient, hessian_weight, psf_tiles, facet_of_row, tile_slot, thresholds):
    band, columns = image_now.shape
    levels = thresholds.shape[0]
    blocks = columns // BLOCK
    scales = lax.axis_size("scales")
    count = lax.axis_size("rows") * scales
    reach = 2 ** (levels + 1) - 2
    side = -(-reach // band)
    own = psf_tiles.reshape(TILE, TILE)
    psf = jnp.stack([own, jnp.flip(own, axis=1)]).reshape(2, TILE * TILE)
    plane = (blocks, WIDTH)
    table = pltpu.VMEM((9, WIDTH, WIDTH), jnp.bfloat16)
    f32 = lambda *shape: pltpu.VMEM(shape, jnp.float32)
    sem = lambda *shape: pltpu.SemaphoreType.DMA(shape)
    smem = pl.BlockSpec(memory_space=pltpu.SMEM)
    exchanges = 3 * SUBITERS - 2
    return pl.pallas_call(
        functools.partial(kernel, count, scales, side),
        out_shape=jax.ShapeDtypeStruct((band, columns), jnp.float32),
        in_specs=[VMEM] * 4 + [smem] * 3 + [VMEM],
        out_specs=VMEM,
        scratch_shapes=[
            f32(*plane), f32(*plane), f32(*plane), f32(*plane),
            f32(exchanges, 2, *plane), f32(*plane), f32(2 * side + 1, *plane),
            f32(count, 2, TILE * TILE), f32(3, 8, TILE * TILE), f32(8, TILE * TILE),
            f32(3 * band, WIDTH), f32(3 * band, WIDTH), table, table, table, table,
            f32(levels, *plane), f32(SUBITERS, count, 2, LANES),
            f32(columns // LANES * 8, LANES), f32(3, 2, WIDTH, LANES),
            sem(count), sem(count), sem(SUBITERS, count), sem(SUBITERS, count), sem(2), sem(2),
            sem(exchanges, 2), sem(exchanges, 2),
            sem(SUBITERS, 2 * side + 1), sem(SUBITERS, 2 * side + 1),
        ],
        compiler_params=pltpu.CompilerParams(
            collective_id=0, has_side_effects=True, vmem_limit_bytes=56 * 1024 * 1024
        ),
    )(image_now, gradient, hessian_weight, psf, facet_of_row, tile_slot, thresholds, spline_matrices(levels))


def solution(mesh):
    band = P(AXES, None)
    in_specs = (band, band, band, band, P(AXES), P(), P())
    return jax.shard_map(body, mesh=mesh, in_specs=in_specs, out_specs=band, check_vma=False)
```

```python
import functools

import jax
import jax.numpy as jnp
import numpy as np
from jax import lax
from jax.experimental import pallas as pl
from jax.experimental.pallas import tpu as pltpu
from jax.sharding import PartitionSpec as P

TILE = 16
HALF = TILE // 2
SUBITERS = 2
LANES = 128
BLOCK = 32
GROUPS = LANES // BLOCK
WIDTH = 8 * BLOCK
AXES = ("rows", "scales")
VMEM = pl.BlockSpec(memory_space=pltpu.VMEM)


def spline_matrices(levels):
    w = np.arange(WIDTH)
    same = (w[:, None] // BLOCK) == (w[None, :] // BLOCK)
    place = w % BLOCK
    nearer = place + np.where(place < BLOCK // 2, BLOCK, -BLOCK)
    planes = []
    for level in range(levels):
        d = 2**level
        for column in (place, nearer):
            o = np.abs(column[:, None] - place[None, :])
            coef = np.where(o == 0, 0.375, np.where(o == d, 0.25, np.where(o == 2 * d, 0.0625, 0.0)))
            planes.append(np.where(same, coef, 0.0))
    return jnp.asarray(np.stack(planes), jnp.bfloat16)


def halves(x):
    high = x.astype(jnp.bfloat16)
    low = (x - high.astype(jnp.float32)).astype(jnp.bfloat16)
    return high, low


def dot(a, b):
    return jnp.dot(a, b, preferred_element_type=jnp.float32)


def block_shift(x, s):
    if s == 0:
        return x
    count = x.shape[0] // GROUPS
    parts = [x[p * count : (p + 1) * count] for p in range(GROUPS)]
    row = lax.broadcasted_iota(jnp.int32, parts[0].shape, 0)
    if s == 1:
        last = jnp.where(row == count - 1, 0.0, pltpu.roll(parts[0], count - 1, 0))
        return jnp.concatenate(parts[1:] + [last], axis=0)
    first = jnp.where(row == 0, 0.0, pltpu.roll(parts[-1], 1, 0))
    return jnp.concatenate([first] + parts[:-1], axis=0)


def beside(x):
    lane = lax.broadcasted_iota(jnp.int32, x.shape, 1) % BLOCK
    return jnp.where(lane < BLOCK // 2, block_shift(x, 1), block_shift(x, -1))


def blur(stripes, high_ref, low_ref):
    total = None
    for t, x in enumerate(stripes):
        for n, y in enumerate((x, beside(x))):
            high, low = halves(y)
            w = high_ref[t * 2 + n]
            part = dot(high, w) + dot(low, w) + dot(high, low_ref[t * 2 + n])
            total = part if total is None else total + part
    return total


def to_blocks(src_ref, dst_ref, tiles):
    count = src_ref.shape[1] // LANES
    for q in range(count):
        tiles[pl.ds(8 * q, 8), :] = src_ref[:, q * LANES : (q + 1) * LANES]
    group = lax.broadcasted_iota(jnp.int32, (count, LANES), 1) // BLOCK
    for half in range(2):
        outs = [None] * GROUPS
        for k in range(4):
            a = tiles[pl.ds(half * 4 + k, count, stride=8), :]
            for p in range(GROUPS):
                shift = BLOCK * ((k - p) % 4)
                moved = pltpu.roll(a, shift, 1) if shift else a
                outs[p] = moved if k == 0 else jnp.where(group == k, moved, outs[p])
        for p in range(GROUPS):
            dst_ref[p * count : (p + 1) * count, half * LANES : (half + 1) * LANES] = outs[p]


def from_blocks(src_ref, dst_ref, tiles):
    count = dst_ref.shape[1] // LANES
    group = lax.broadcasted_iota(jnp.int32, (count, LANES), 1) // BLOCK
    for half in range(2):
        for k in range(4):
            out = None
            for p in range(GROUPS):
                x = src_ref[p * count : (p + 1) * count, half * LANES : (half + 1) * LANES]
                shift = BLOCK * ((p - k) % 4)
                moved = pltpu.roll(x, shift, 1) if shift else x
                out = moved if p == 0 else jnp.where(group == p, moved, out)
            tiles[pl.ds(half * 4 + k, count, stride=8), :] = out
    for q in range(count):
        dst_ref[:, q * LANES : (q + 1) * LANES] = tiles[pl.ds(8 * q, 8), :]


def build_weights(base_ref, lead, high_ref, low_ref, wide):
    lane = lax.broadcasted_iota(jnp.int32, (8, WIDTH), 1) % BLOCK
    for t in range(3):
        base = base_ref[8 * t : 8 * t + 8, :]
        for w in range(BLOCK):
            for n, s in enumerate((0, 1 if w < BLOCK // 2 else -1)):
                moved = pltpu.roll(base, (w - lead + BLOCK * s) % WIDTH, 1)
                x = lane - (w - lead + BLOCK * s)
                kept = jnp.where((x >= 0) & (x < TILE), moved, 0.0)
                for half in range(2):
                    wide[n, half, pl.ds(w, 8, stride=BLOCK), :] = kept[
                        :, half * LANES : (half + 1) * LANES
                    ]
        for n in range(2):
            for half in range(2):
                high, low = halves(wide[n, half])
                high_ref[t * 2 + n, :, half * LANES : (half + 1) * LANES] = high
                low_ref[t * 2 + n, :, half * LANES : (half + 1) * LANES] = low


def moved_rows(vregs, rolls, i, d):
    if d % 4 == 0:
        return vregs[i + d // 4]
    shift = (-BLOCK * d) % LANES

    def rolled(n):
        if (n, shift) not in rolls:
            rolls[(n, shift)] = pltpu.roll(vregs[n], shift, 1)
        return rolls[(n, shift)]

    lane = lax.broadcasted_iota(jnp.int32, vregs[i].shape, 1)
    if d > 0:
        return jnp.where(lane < LANES - BLOCK * d, rolled(i), rolled(i + 1))
    return jnp.where(lane >= -BLOCK * d, rolled(i), rolled(i - 1))


def column_cascade(images, descents, step, alive, levels_ref, step_rows):
    reach = images.shape[0] // 2
    wide_step = jnp.broadcast_to(step, (step_rows, LANES))
    levels = levels_ref.shape[0]

    def chunk(n, carry):
        rows = pl.ds(pl.multiple_of(n * step_rows, step_rows), step_rows)
        vregs = {}
        for t in range(images.shape[0]):
            for half in range(2):
                lanes = slice(half * LANES, (half + 1) * LANES)
                vregs[2 * t + half] = images[t, rows, lanes] - wide_step * descents[t, rows, lanes]
        own = 2 * reach
        for level in range(levels):
            d = 2**level
            left = 2 ** (levels + 1) - 2 ** (level + 2)
            margin = -(-left // 4)
            rolls, out = {}, {}
            keys = vregs
            for i in range(own - margin, own + 2 + margin):
                outer = moved_rows(keys, rolls, i, -2 * d) + moved_rows(keys, rolls, i, 2 * d)
                inner = moved_rows(keys, rolls, i, -d) + moved_rows(keys, rolls, i, d)
                value = 0.0625 * outer + 0.25 * inner + 0.375 * keys[i]
                t = i // 2
                out[i] = value if t == reach else value * alive[t]
            vregs = out
            for half in range(2):
                levels_ref[level, rows, half * LANES : (half + 1) * LANES] = out[own + half]
        return carry

    lax.fori_loop(0, images.shape[1] // step_rows, chunk, 0)


def row_cascade(levels_ref, spline_ref):
    levels = levels_ref.shape[0]
    for level in range(levels):

        def one(k, carry):
            x = levels_ref[k]
            total = None
            for n, y in enumerate((x, beside(x))):
                high, low = halves(y)
                w = spline_ref[level * 2 + n]
                part = dot(high, w) + dot(low, w)
                total = part if total is None else total + part
            levels_ref[k] = total
            return carry

        lax.fori_loop(level, levels, one, 0)


def keep(own, levels_ref, limits):
    levels = levels_ref.shape[0]
    smooth = own
    total = None
    for k in range(levels):
        smoother = levels_ref[k]
        detail = smooth - smoother
        part = detail - jnp.clip(detail, -limits[k], limits[k])
        total = part if total is None else total + part
        smooth = smoother
    return total + smooth


def build_bases(taps, flipped, forward, adjoint):
    lane = lax.broadcasted_iota(jnp.int32, (8, WIDTH), 1)
    sub = lax.broadcasted_iota(jnp.int32, (8, WIDTH), 0)
    group, inside = lane // BLOCK, lane % BLOCK < TILE
    own = flipped[...]
    turned = [pltpu.roll(own, TILE * n, 1) if n else own for n in range(TILE)]
    forward[...] = jnp.zeros_like(forward)
    for a in range(TILE):
        placed = jnp.zeros((8, WIDTH), jnp.float32)
        for r in range(8):
            placed = jnp.where((sub == r) & (group == r) & inside, turned[(2 * r - a) % TILE], placed)
        forward[a : a + 8, :] += placed
    for t in range(3):
        x = taps[t]
        row = sub + 8 * t
        tap = group - row + TILE
        placed = jnp.zeros((8, WIDTH), jnp.float32)
        for n in range(TILE):
            moved = pltpu.roll(x, TILE * n, 1) if n else x
            use = ((group + row) % TILE == n) & inside & (tap >= 0) & (tap < TILE)
            placed = jnp.where(use, moved, placed)
        adjoint[8 * t : 8 * t + 8, :] = placed


def kernel(
    count, scales, side,
    image, gradient, weight, psf, facet, slot_of, thresholds, spline,
    out,
    xh, current, near, far, psf_all, taps, flipped, base_f, base_a, fh, fl, ah, al,
    levels, sums, tiles, wide,
    psf_send, psf_recv, sum_send, sum_recv, tap_send, tap_recv, near_send, near_recv, far_send, far_recv,
):
    me = lax.axis_index("rows") * scales + lax.axis_index("scales")
    barrier = pltpu.get_barrier_semaphore()

    def device(index):
        return (index // scales, index % scales)

    def peer(k):
        return (me + k) % count

    def exists(o):
        return (me + o >= 0) & (me + o < count)

    def greet(k, carry):
        pl.semaphore_signal(barrier, inc=1, device_id=device(peer(k)), device_id_type=MESH)
        return carry

    lax.fori_loop(1, count, greet, 0)

    def copy(src, dst, send_sem, recv_sem, index):
        return pltpu.make_async_remote_copy(
            src_ref=src, dst_ref=dst, send_sem=send_sem, recv_sem=recv_sem,
            device_id=device(index), device_id_type=MESH,
        )

    def share(src, pool, send, recv):
        def start(k, carry):
            copy(src, pool.at[me], send.at[k], recv.at[me], peer(k)).start()
            return carry

        lax.fori_loop(1, count, start, 0)

    def collect(src, pool, send, recv):
        def wait(k, carry):
            copy(src, pool.at[peer(k)], send.at[k], recv.at[peer(k)], peer(k)).wait()
            return carry

        lax.fori_loop(1, count, wait, 0)

    def spread(src, place, send, recv, offsets):
        for o in offsets:

            @pl.when(exists(o))
            def _():
                copy(src, place(-o), send(o), recv(-o), me + o).start()

    def arrive(src, place, send, recv, offsets):
        for o in offsets:

            @pl.when(exists(o))
            def _():
                copy(src, place(o), send(o), recv(o), me + o).wait()

    def pushed_args(e, src):
        return (src, lambda o: near.at[e, (o + 1) // 2], lambda o: near_send.at[e, (o + 1) // 2],
                lambda o: near_recv.at[e, (o + 1) // 2], close)

    close = [-1, 1]
    distant = [sign * o for o in range(2, side + 1) for sign in (-1, 1)]

    def plane_args(e, offsets):
        return (far.at[e, side], lambda o: far.at[e, o + side], lambda o: far_send.at[e, o + side],
                lambda o: far_recv.at[e, o + side], offsets)

    to_blocks(gradient, far.at[1, side], tiles)
    to_blocks(image, far.at[0, side], tiles)
    for o in close:

        @pl.when(jnp.logical_not(exists(o)))
        def _():
            for e in range(near.shape[0]):
                near[e, (o + 1) // 2] = jnp.zeros(near.shape[2:], jnp.float32)
            taps[o + 1] = jnp.zeros(taps.shape[1:], jnp.float32)

    for o in close + distant:

        @pl.when(jnp.logical_not(exists(o)))
        def _():
            for e in range(far.shape[0]):
                far[e, o + side] = jnp.zeros(far.shape[2:], jnp.float32)

    pl.semaphore_wait(barrier, count - 1)
    share(psf, psf_all, psf_send, psf_recv)
    spread(*plane_args(1, close))
    spread(*plane_args(0, close))
    spread(*plane_args(1, distant))
    spread(*plane_args(0, distant))
    to_blocks(weight, xh, tiles)
    psf_all[me] = psf[...]
    collect(psf, psf_all, psf_send, psf_recv)
    for r in range(8):
        both = psf_all[slot_of[facet[r]]]
        taps[1, r : r + 1, :] = both[0:1]
        flipped[r : r + 1, :] = both[1:2]
    tap_args = (taps.at[1], lambda o: taps.at[o + 1], lambda o: tap_send.at[(o + 1) // 2],
                lambda o: tap_recv.at[(o + 1) // 2], (-1, 1))
    spread(*tap_args)
    arrive(*tap_args)
    build_bases(taps, flipped, base_f, base_a)
    build_weights(base_f, HALF - 1, fh, fl, wide)
    alive = [None if t == side else jnp.where(exists(t - side), 1.0, 0.0) for t in range(2 * side + 1)]

    for sweep in range(SUBITERS):
        e = 2 * sweep
        if sweep > 0:
            images = [far[0, side + o] for o in (-1, 0, 1)]
            arrive(*plane_args(e, close))
            changes = [far[e, side + o] - images[o + 1] for o in (-1, 0, 1)]
            current[...] = xh[...] * blur(changes, fh, fl)
            args = pushed_args(sweep - 1, current)
            spread(*args)
            spread(*plane_args(e, distant))
            arrive(*args)
            pushed = [near[sweep - 1, 0], current[...], near[sweep - 1, 1]]
            far[e + 1, side] = far[1, side] + blur(pushed, ah, al)
            spread(*plane_args(e + 1, close))
            spread(*plane_args(e + 1, distant))
        arrive(*plane_args(e + 1, close))
        d = far[e + 1, side]
        b = blur([far[e + 1, side - 1], d, far[e + 1, side + 1]], fh, fl)

        def lanes(x):
            column = jnp.sum(x, axis=0, keepdims=True)
            return column[:, :LANES] + column[:, LANES:]

        sums[sweep, me] = jnp.concatenate([lanes(d * d), lanes(xh[...] * b * b)], axis=0)
        own = sums.at[sweep, me]
        share(own, sums.at[sweep], sum_send.at[sweep], sum_recv.at[sweep])
        if sweep == 0:
            build_weights(base_a, HALF, ah, al, wide)
        collect(own, sums.at[sweep], sum_send.at[sweep], sum_recv.at[sweep])
        totals = jnp.sum(jnp.sum(sums[sweep], axis=0), axis=1, keepdims=True)
        step = totals[0:1] / totals[1:2]
        if sweep == 0:
            arrive(*plane_args(e, close))
        arrive(*plane_args(e, distant))
        arrive(*plane_args(e + 1, distant))
        column_cascade(far.at[e], far.at[e + 1], step, alive, levels, 8)
        row_cascade(levels, spline)
        trial = far[e, side] - step * far[e + 1, side]
        new = keep(trial, levels, [step * thresholds[k] for k in range(levels.shape[0])])
        if sweep < SUBITERS - 1:
            far[e + 2, side] = new
            spread(*plane_args(e + 2, close))
        else:
            current[...] = new
    from_blocks(current, out, tiles)


MESH = pl.DeviceIdType.MESH


def body(image_now, gradient, hessian_weight, psf_tiles, facet_of_row, tile_slot, thresholds):
    band, columns = image_now.shape
    levels = thresholds.shape[0]
    blocks = columns // BLOCK
    scales = lax.axis_size("scales")
    count = lax.axis_size("rows") * scales
    reach = 2 ** (levels + 1) - 2
    side = -(-reach // band)
    own = psf_tiles.reshape(TILE, TILE)
    psf = jnp.stack([own, jnp.flip(own, axis=1)]).reshape(2, TILE * TILE)
    plane = (blocks, WIDTH)
    table = pltpu.VMEM((6, WIDTH, WIDTH), jnp.bfloat16)
    f32 = lambda *shape: pltpu.VMEM(shape, jnp.float32)
    sem = lambda *shape: pltpu.SemaphoreType.DMA(shape)
    smem = pl.BlockSpec(memory_space=pltpu.SMEM)
    pairs = 2 * SUBITERS
    return pl.pallas_call(
        functools.partial(kernel, count, scales, side),
        out_shape=jax.ShapeDtypeStruct((band, columns), jnp.float32),
        in_specs=[VMEM] * 4 + [smem] * 3 + [VMEM],
        out_specs=VMEM,
        scratch_shapes=[
            f32(*plane), f32(*plane),
            f32(SUBITERS - 1, 2, *plane), f32(pairs, 2 * side + 1, *plane),
            f32(count, 2, TILE * TILE), f32(3, 8, TILE * TILE), f32(8, TILE * TILE),
            f32(3 * band, WIDTH), f32(3 * band, WIDTH), table, table, table, table,
            f32(levels, *plane), f32(SUBITERS, count, 2, LANES),
            f32(columns // LANES * 8, LANES), f32(2, 2, WIDTH, LANES),
            sem(count), sem(count), sem(SUBITERS, count), sem(SUBITERS, count), sem(2), sem(2),
            sem(SUBITERS - 1, 2), sem(SUBITERS - 1, 2),
            sem(pairs, 2 * side + 1), sem(pairs, 2 * side + 1),
        ],
        compiler_params=pltpu.CompilerParams(
            collective_id=0, has_side_effects=True, vmem_limit_bytes=56 * 1024 * 1024
        ),
    )(image_now, gradient, hessian_weight, psf, facet_of_row, tile_slot, thresholds, spline_matrices(levels))


def solution(mesh):
    band = P(AXES, None)
    in_specs = (band, band, band, band, P(AXES), P(), P())
    return jax.shard_map(body, mesh=mesh, in_specs=in_specs, out_specs=band, check_vma=False)
```
